32 devices in a mesh: dp: 8 (over y, x, core), ctx: 4 (over z).
Axes of the slice: x: 2, y: 2, z: 4, core: 2. Of those that a mesh axis runs over, the one named last changes fastest.
Arguments:
- layer_input: bfloat16 [4096, 768], P(('dp', 'ctx')), may hold values from -6 to 6
- lengths: int32 [8], P('dp'), may hold values from 128 to 512, as said below
- qkv_weight: bfloat16 [768, 2304], P(('dp', 'ctx')), may hold values from -1 to 1
- qv_bias: bfloat16 [1536], P(('dp', 'ctx')), may hold values from -3 to 3
- out_weight: bfloat16 [768, 768], P(('dp', 'ctx')), may hold values from -1.75 to 1.75
- out_bias: bfloat16 [768], P(('dp', 'ctx')), may hold values from -3 to 3
- first_gain: bfloat16 [768], P(('dp', 'ctx')), may hold values from 0.099609375 to 1.8984375
- first_shift: bfloat16 [768], P(('dp', 'ctx')), may hold values from -3 to 3
- up_weight: bfloat16 [768, 3072], P(('dp', 'ctx')), may hold values from -0.21875 to 0.21875
- up_bias: bfloat16 [3072], P(('dp', 'ctx')), may hold values from -3 to 3
- down_weight: bfloat16 [3072, 768], P(('dp', 'ctx')), may hold values from -0.109375 to 0.109375
- down_bias: bfloat16 [768], P(('dp', 'ctx')), may hold values from -3 to 3
- second_gain: bfloat16 [768], P(('dp', 'ctx')), may hold values from 0.099609375 to 1.8984375
- second_shift: bfloat16 [768], P(('dp', 'ctx')), may hold values from -3 to 3
- cotangent: bfloat16 [4096, 768], P(('dp', 'ctx')), may hold values from -6 to 6
Outputs:
- layer_output: bfloat16 [4096, 768], P(('dp', 'ctx'))
- input_grad: float32 [4096, 768], P(('dp', 'ctx'))
- qkv_weight_grad: float32 [768, 2304], P(('dp', 'ctx'))
- qv_bias_grad: float32 [1536], P(('dp', 'ctx'))
- out_weight_grad: float32 [768, 768], P(('dp', 'ctx'))
- out_bias_grad: float32 [768], P(('dp', 'ctx'))
- first_gain_grad: float32 [768], P(('dp', 'ctx'))
- first_shift_grad: float32 [768], P(('dp', 'ctx'))
- up_weight_grad: float32 [768, 3072], P(('dp', 'ctx'))
- up_bias_grad: float32 [3072], P(('dp', 'ctx'))
- down_weight_grad: float32 [3072, 768], P(('dp', 'ctx'))
- down_bias_grad: float32 [768], P(('dp', 'ctx'))
- second_gain_grad: float32 [768], P(('dp', 'ctx'))
- second_shift_grad: float32 [768], P(('dp', 'ctx'))
The draws below stay inside these ranges and needn't reach their ends.
Inputs may be any that keep to these rules, and one draw needn't show every extreme that they name: `lengths`: each entry is one of the 512 positions or fewer, some sequence has all 512 valid.
All inputs are finite; a program needn't handle non-finite values.
Results may differ from the reference program's by a relative error of at most 0.014.
The reference program's roundings to bfloat16 on the way count: a program that leaves them out, or rounds other values in their place, can miss the bound.
Values may be sent and summed in bfloat16 or wider, within the bound.
A program may use at most 192 MiB of HBM per device.

```python
import jax
import jax.numpy as jnp
from jax import lax

D = 768
HEAD_DIM = 64
FF = 3072
SEQ_LEN = 512
SEQS = 8
TOKENS = 4096


def draw_layer_input(key, part):
    values = jax.random.normal(key, (TOKENS, D), jnp.float32)
    return jnp.clip(values, -6.0, 6.0).astype(jnp.bfloat16)


def draw_qkv_weight(key, part):
    base = jnp.clip(jax.random.normal(key, (D, 3 * D), jnp.float32), -6.0, 6.0) * D ** (-0.5)
    return base.astype(jnp.bfloat16)


def draw_lengths(key, part):
    drawn = jax.random.randint(key, (SEQS,), SEQ_LEN // 4, SEQ_LEN + 1)
    place = jax.random.randint(jax.random.fold_in(key, 5), (), 0, SEQS)
    return jnp.where(jnp.arange(SEQS) == place, SEQ_LEN, drawn).astype(jnp.int32)


def raised(values, key, source, target, blocks, factor):
    def block_of(dim):
        return (jnp.arange(values.shape[dim]) // (values.shape[dim] // blocks)).reshape((-1,) + (1,) * (values.ndim - 1 - dim))

    first = jax.random.permutation(key, blocks)[block_of(target)]
    other_side = (block_of(target) + blocks // 2) % blocks
    return jnp.where((block_of(source) == first) | (block_of(source) == other_side), factor * values, values)


def shard_levels(stream_key, extent, shards, low, high):
    loudness, own = 1.0, jax.random.fold_in(stream_key, 6)
    for dim, shards_of in shards:
        steps = jnp.exp(jax.random.uniform(jax.random.fold_in(own, dim), (shards_of,), jnp.float32, low / len(shards), high / len(shards)))
        loudness = loudness * jnp.repeat(steps, extent[dim] // shards_of).reshape([-1 if axis == dim else 1 for axis in range(len(extent))])
    return loudness


def noise(stream_key, extent, scale, reach, cuts=(), held_as=jnp.bfloat16):
    values = jax.random.normal(stream_key, extent, jnp.float32) * scale
    if len(cuts) > 0:
        values = shard_levels(stream_key, extent, cuts, -0.22, 0.18) * values
    return jnp.clip(values, min=-reach, max=reach).astype(held_as)


def bell_draw_with(key, dims, scale, reach, cuts, heavy, kind=jnp.bfloat16):
    values = scale * jax.random.normal(key, dims, jnp.float32)
    if cuts:
        values = values * shard_levels(key, dims, cuts, -0.22, 0.18)
    return jnp.clip(raised(values, jax.random.fold_in(key, 3), *heavy), -reach, reach).astype(kind)


def setup_inputs(seed: int = 0) -> dict:
    key_list = jax.random.split(jax.random.key(seed), 16)
    layer_input = draw_layer_input(jax.random.fold_in(key_list[15], 71), 0)
    lengths = draw_lengths(jax.random.fold_in(key_list[15], 71), 0)
    qkv_weight = draw_qkv_weight(jax.random.fold_in(key_list[15], 71), 0)
    qv_bias = noise(key_list[3], (2 * D,), 0.5, 3.0, ((0, 32),))
    out_weight = noise(key_list[4], (D, D), (D // 64) ** -0.5, 1.75, ((0, 32),))
    out_bias = noise(key_list[5], (D,), 0.5, 3.0, ((0, 32),))
    first_gain = jnp.clip(1.0 + 0.18 * jax.random.normal(key_list[6], (D,), jnp.float32), 0.099609375, 1.8984375).astype(jnp.bfloat16)
    first_shift = noise(key_list[7], (D,), 0.5, 3.0, ((0, 32),))
    up_weight = noise(key_list[8], (D, FF), D ** -0.5, 0.21875, ((0, 32),))
    up_bias = noise(key_list[9], (FF,), 0.5, 3.0, ((0, 32),))
    down_weight = noise(key_list[10], (FF, D), FF ** -0.5, 0.109375, ((0, 32),))
    down_bias = noise(key_list[11], (D,), 0.5, 3.0, ((0, 32),))
    second_gain = jnp.clip(1.0 + 0.18 * jax.random.normal(key_list[12], (D,), jnp.float32), 0.099609375, 1.8984375).astype(jnp.bfloat16)
    second_shift = noise(key_list[13], (D,), 0.5, 3.0, ((0, 32),))
    cotangent = bell_draw_with(key_list[14], (TOKENS, D), 1.0, 6.0, ((0, 32),), (0, 1, 32, 2.75))
    return dict(layer_input=layer_input, lengths=lengths, qkv_weight=qkv_weight, qv_bias=qv_bias, out_weight=out_weight, out_bias=out_bias, first_gain=first_gain, first_shift=first_shift, up_weight=up_weight, up_bias=up_bias, down_weight=down_weight, down_bias=down_bias, second_gain=second_gain, second_shift=second_shift, cotangent=cotangent)


EPSILON = 1e-05

def gelu_tanh(value):
    return 0.5 * value * (1.0 + jnp.tanh(0.7978845608028654 * (value + 0.044715 * value * value * value)))

def widen(array):
    return lax.optimization_barrier(array).astype(jnp.float32)

def product(left, right):
    return jnp.dot(left, right, preferred_element_type=jnp.float32)

def product_tn(left, right):
    return lax.dot_general(left, right, (((0,), (0,)), ((), ())), preferred_element_type=jnp.float32)

def product_nt(left, right):
    return lax.dot_general(left, right, (((1,), (1,)), ((), ())), preferred_element_type=jnp.float32)

def norm_forward(rows, gain, shift):
    centered = rows - lax.optimization_barrier(jnp.mean(rows, axis=-1, keepdims=True))
    inverse = lax.rsqrt(lax.optimization_barrier(jnp.mean(centered * centered, axis=-1, keepdims=True)) + EPSILON)
    normed = centered * inverse
    return (normed * gain + shift, normed, inverse)

def norm_backward(grad_rows, normed, inverse, gain):
    scaled = grad_rows * gain
    return inverse * (scaled - lax.optimization_barrier(jnp.mean(scaled, axis=-1, keepdims=True)) - normed * lax.optimization_barrier(jnp.mean(scaled * normed, axis=-1, keepdims=True)))

def split_heads(array):
    return widen(array).reshape(array.shape[0], 2, HEAD_DIM)

def pair_scores(query_pair, key_pair, key_valid):
    scores = jnp.einsum('qhd,khd->hqk', split_heads(query_pair), split_heads(key_pair)) * HEAD_DIM ** (-0.5)
    return jnp.where(key_valid[None, None, :], scores, -jnp.inf)

def attention_forward(queries, keys_all, values_all, key_valid):
    outputs = []
    totals = []
    for pair_index in range(queries.shape[1] // (2 * HEAD_DIM)):
        offset = pair_index * 2 * HEAD_DIM
        columns = slice(offset, offset + 2 * HEAD_DIM)
        scores = pair_scores(queries[:, columns], keys_all[:, columns], key_valid)
        row_peak = lax.optimization_barrier(jnp.max(scores, axis=-1, keepdims=True))
        log_total = row_peak + jnp.log(lax.optimization_barrier(jnp.sum(jnp.exp(scores - row_peak), axis=-1, keepdims=True)))
        attn_weights = jnp.exp(scores - log_total).astype(jnp.bfloat16)
        mixed_heads = jnp.einsum('hqk,khd->qhd', widen(attn_weights), split_heads(values_all[:, columns]))
        outputs.append(mixed_heads.reshape(mixed_heads.shape[0], 2 * HEAD_DIM))
        totals.append(log_total)
    return (jnp.concatenate(outputs, axis=1), totals)

def attention_backward(queries, keys_all, values_all, key_valid, totals, grad_attended):
    grad_q_list = []
    grad_k_list = []
    grad_v_list = []
    for pair_index in range(queries.shape[1] // (2 * HEAD_DIM)):
        offset = pair_index * 2 * HEAD_DIM
        columns = slice(offset, offset + 2 * HEAD_DIM)
        scores = pair_scores(queries[:, columns], keys_all[:, columns], key_valid)
        probs = jnp.exp(scores - totals[pair_index])
        probs_low = probs.astype(jnp.bfloat16)
        heads_grad = split_heads(grad_attended[:, columns])
        grad_values = jnp.einsum('hqk,qhd->khd', widen(probs_low), heads_grad)
        grad_probs = jnp.einsum('qhd,khd->hqk', heads_grad, split_heads(values_all[:, columns]))
        grad_scores = probs * (grad_probs - lax.optimization_barrier(jnp.sum(probs * grad_probs, axis=-1, keepdims=True)))
        grad_low = widen(grad_scores.astype(jnp.bfloat16))
        grad_queries = jnp.einsum('hqk,khd->qhd', grad_low, split_heads(keys_all[:, columns])) * HEAD_DIM ** (-0.5)
        grad_keys = jnp.einsum('hqk,qhd->khd', grad_low, split_heads(queries[:, columns])) * HEAD_DIM ** (-0.5)
        grad_q_list.append(grad_queries.reshape(grad_queries.shape[0], 2 * HEAD_DIM))
        grad_k_list.append(grad_keys.reshape(grad_keys.shape[0], 2 * HEAD_DIM))
        grad_v_list.append(grad_values.reshape(grad_values.shape[0], 2 * HEAD_DIM))
    return (jnp.concatenate(grad_q_list, axis=1), jnp.concatenate(grad_k_list, axis=1), jnp.concatenate(grad_v_list, axis=1))

def sequence_layer(seq_input, seq_cot, seq_length, params):
    qkv_weight, qv_bias, out_weight, out_bias, first_gain, first_shift, up_weight, up_bias, down_weight, down_bias, second_gain, second_shift = params
    width = seq_input.shape[1]
    joined = product(seq_input, qkv_weight)
    bias_wide = qv_bias.astype(jnp.float32)
    queries = (joined[:, :width] + bias_wide[:width]).astype(jnp.bfloat16)
    keys_all = joined[:, width:2 * width].astype(jnp.bfloat16)
    values_all = (joined[:, 2 * width:] + bias_wide[width:]).astype(jnp.bfloat16)
    key_valid = jnp.arange(seq_input.shape[0], dtype=jnp.int32) < seq_length
    attended, totals = attention_forward(queries, keys_all, values_all, key_valid)
    attended_low = attended.astype(jnp.bfloat16)
    first_sum = seq_input.astype(jnp.float32) + product(attended_low, out_weight) + out_bias.astype(jnp.float32)
    gain_one = first_gain.astype(jnp.float32)
    hidden, normed_first, inverse_first = norm_forward(first_sum, gain_one, first_shift.astype(jnp.float32))
    hidden_low = hidden.astype(jnp.bfloat16)
    upper = product(hidden_low, up_weight) + up_bias.astype(jnp.float32)
    activation, gelu_back = jax.vjp(gelu_tanh, upper)
    activation_low = activation.astype(jnp.bfloat16)
    second_sum = hidden + product(activation_low, down_weight) + down_bias.astype(jnp.float32)
    gain_two = second_gain.astype(jnp.float32)
    result, normed_second, inverse_second = norm_forward(second_sum, gain_two, second_shift.astype(jnp.float32))
    layer_output = result.astype(jnp.bfloat16)
    cot_wide = seq_cot.astype(jnp.float32)
    second_shift_grad = lax.optimization_barrier(jnp.sum(cot_wide, axis=0))
    second_gain_grad = lax.optimization_barrier(jnp.sum(cot_wide * normed_second, axis=0))
    grad_second = norm_backward(cot_wide, normed_second, inverse_second, gain_two)
    down_bias_grad = lax.optimization_barrier(jnp.sum(grad_second, axis=0))
    grad_second_low = grad_second.astype(jnp.bfloat16)
    down_weight_grad = product_tn(activation_low, grad_second_low)
    grad_upper = gelu_back(product_nt(grad_second_low, down_weight))[0]
    up_bias_grad = lax.optimization_barrier(jnp.sum(grad_upper, axis=0))
    grad_upper_low = grad_upper.astype(jnp.bfloat16)
    up_weight_grad = product_tn(hidden_low, grad_upper_low)
    grad_hidden = grad_second + product_nt(grad_upper_low, up_weight)
    first_shift_grad = lax.optimization_barrier(jnp.sum(grad_hidden, axis=0))
    first_gain_grad = lax.optimization_barrier(jnp.sum(grad_hidden * normed_first, axis=0))
    grad_first = norm_backward(grad_hidden, normed_first, inverse_first, gain_one)
    out_bias_grad = lax.optimization_barrier(jnp.sum(grad_first, axis=0))
    grad_first_low = grad_first.astype(jnp.bfloat16)
    out_weight_grad = product_tn(attended_low, grad_first_low)
    grad_attended = product_nt(grad_first_low, out_weight).astype(jnp.bfloat16)
    grad_queries, grad_keys, grad_values = attention_backward(queries, keys_all, values_all, key_valid, totals, grad_attended)
    qv_bias_grad = jnp.concatenate([lax.optimization_barrier(jnp.sum(grad_queries, axis=0)), lax.optimization_barrier(jnp.sum(grad_values, axis=0))])
    grad_joined = jnp.concatenate([grad_queries, grad_keys, grad_values], axis=1).astype(jnp.bfloat16)
    qkv_weight_grad = product_tn(seq_input, grad_joined)
    input_grad = grad_first + product_nt(grad_joined, qkv_weight)
    grads = (qkv_weight_grad, qv_bias_grad, out_weight_grad, out_bias_grad, first_gain_grad, first_shift_grad, up_weight_grad, up_bias_grad, down_weight_grad, down_bias_grad, second_gain_grad, second_shift_grad)
    return (layer_output, input_grad, grads)

def reference(layer_input, lengths, qkv_weight, qv_bias, out_weight, out_bias, first_gain, first_shift, up_weight, up_bias, down_weight, down_bias, second_gain, second_shift, cotangent):
    width = layer_input.shape[1]
    seq_count = lengths.shape[0]
    params = (qkv_weight, qv_bias, out_weight, out_bias, first_gain, first_shift, up_weight, up_bias, down_weight, down_bias, second_gain, second_shift)
    inputs_seq = layer_input.reshape(seq_count, -1, width)
    cot_seq = cotangent.reshape(seq_count, -1, width)

    def one_step(carry, items):
        seq_input, seq_cot, seq_length = items
        output_rows, grad_rows, grads = sequence_layer(seq_input, seq_cot, seq_length, params)
        return (jax.tree.map(jnp.add, carry, grads), (output_rows, grad_rows))
    zeros = tuple((jnp.zeros(param.shape, jnp.float32) for param in params))
    totals, (outputs, in_grads) = lax.scan(one_step, zeros, (inputs_seq, cot_seq, lengths))
    return (outputs.reshape(-1, width), in_grads.reshape(-1, width), totals[0], totals[1], totals[2], totals[3], totals[4], totals[5], totals[6], totals[7], totals[8], totals[9], totals[10], totals[11])
```

```python
import jax
import jax.numpy as jnp
from jax import lax
from jax.experimental import pallas as pl
from jax.experimental.pallas import tpu as pltpu
from jax.sharding import PartitionSpec as P

HEAD_DIM = 64


EPSILON = 1e-05


def gelu_tanh(value):
    return (
        0.5
        * value
        * (1.0 + jnp.tanh(0.7978845608028654 * (value + 0.044715 * value * value * value)))
    )


def product(left, right):
    return jnp.dot(left, right, preferred_element_type=jnp.float32)


def product_tn(left, right):
    return lax.dot_general(
        left, right, (((0,), (0,)), ((), ())), preferred_element_type=jnp.float32
    )


def product_nt(left, right):
    return lax.dot_general(
        left, right, (((1,), (1,)), ((), ())), preferred_element_type=jnp.float32
    )


def norm_forward(rows, gain, shift):
    centered = rows - jnp.mean(rows, axis=-1, keepdims=True)
    inverse = lax.rsqrt(jnp.mean(centered * centered, axis=-1, keepdims=True) + EPSILON)
    normed = centered * inverse
    return (normed * gain + shift, normed, inverse)


def norm_backward(grad_rows, normed, inverse, gain):
    scaled = grad_rows * gain
    return inverse * (
        scaled
        - jnp.mean(scaled, axis=-1, keepdims=True)
        - normed * jnp.mean(scaled * normed, axis=-1, keepdims=True)
    )


LANES = 128
AXES = ("dp", "ctx")


def head_scores(query, key, limit):
    scores = product_nt(query, key) * HEAD_DIM ** (-0.5)
    position = lax.broadcasted_iota(jnp.int32, scores.shape, 1)
    return jnp.where(position < limit, scores, -jnp.inf)


def log_sum(scores):
    peak = jnp.max(scores, axis=-1, keepdims=True)
    return peak + jnp.log(jnp.sum(jnp.exp(scores - peak), axis=-1, keepdims=True))


def forward_kernel(length_ref, query_ref, key_ref, value_ref, out_ref):
    limit = length_ref[0]
    for head in range(LANES // HEAD_DIM):
        span = slice(head * HEAD_DIM, (head + 1) * HEAD_DIM)
        scores = head_scores(query_ref[:, span], key_ref[:, span], limit)
        weights = jnp.exp(scores - log_sum(scores)).astype(jnp.bfloat16)
        out_ref[:, span] = product(weights, value_ref[:, span]).astype(jnp.bfloat16)


def backward_kernel(
    length_ref, query_ref, key_ref, value_ref, grad_ref, gq_ref, gk_ref, gv_ref, qsum_ref, vsum_ref
):
    limit = length_ref[0]
    scale = HEAD_DIM ** (-0.5)
    for head in range(LANES // HEAD_DIM):
        span = slice(head * HEAD_DIM, (head + 1) * HEAD_DIM)
        query, key, value = query_ref[:, span], key_ref[:, span], value_ref[:, span]
        grad = grad_ref[:, span]
        scores = head_scores(query, key, limit)
        probs = jnp.exp(scores - log_sum(scores))
        grad_probs = product_nt(grad, value)
        inner = jnp.sum(probs * grad_probs, axis=-1, keepdims=True)
        grad_low = (probs * (grad_probs - inner)).astype(jnp.bfloat16)
        grad_query = product(grad_low, key) * scale
        gq_ref[:, span] = grad_query.astype(jnp.bfloat16)
        gk_ref[:, span] = (product_tn(grad_low, query) * scale).astype(jnp.bfloat16)
        grad_value = product_tn(probs.astype(jnp.bfloat16), grad)
        gv_ref[:, span] = grad_value.astype(jnp.bfloat16)
        qsum_ref[:, span] = jnp.broadcast_to(
            jnp.sum(grad_query, axis=0, keepdims=True), (8, HEAD_DIM)
        )
        vsum_ref[:, span] = jnp.broadcast_to(
            jnp.sum(grad_value, axis=0, keepdims=True), (8, HEAD_DIM)
        )


def attention_specs(rows, total, pairs):
    local = pl.BlockSpec((rows, LANES), lambda p: (0, p))
    return (
        pl.BlockSpec(memory_space=pltpu.SMEM),
        local,
        pl.BlockSpec((total, LANES), lambda p: (0, p)),
        pl.BlockSpec((total, LANES), lambda p: (0, pairs + p)),
    )


def attention_forward(lengths, queries, keys_values):
    rows, width = queries.shape
    total, pairs = keys_values.shape[0], width // LANES
    work = 4 * rows * total * width
    return pl.pallas_call(
        forward_kernel,
        grid=(pairs,),
        in_specs=attention_specs(rows, total, pairs),
        out_specs=pl.BlockSpec((rows, LANES), lambda p: (0, p)),
        out_shape=jax.ShapeDtypeStruct((rows, width), jnp.bfloat16),
        cost_estimate=pl.CostEstimate(
            flops=work, bytes_accessed=4 * total * width, transcendentals=work // 64
        ),
        name="attend_forward",
    )(lengths, queries, keys_values, keys_values)


def attention_backward(lengths, queries, keys_values, grad_attended):
    rows, width = queries.shape
    total, pairs = keys_values.shape[0], width // LANES
    work = 10 * rows * total * width
    local = pl.BlockSpec((rows, LANES), lambda p: (0, p))
    long = pl.BlockSpec((total, LANES), lambda p: (0, p))
    short = pl.BlockSpec((8, LANES), lambda p: (0, p))
    return pl.pallas_call(
        backward_kernel,
        grid=(pairs,),
        in_specs=(*attention_specs(rows, total, pairs), local),
        out_specs=(local, long, long, short, short),
        out_shape=(
            jax.ShapeDtypeStruct((rows, width), jnp.bfloat16),
            jax.ShapeDtypeStruct((total, width), jnp.bfloat16),
            jax.ShapeDtypeStruct((total, width), jnp.bfloat16),
            jax.ShapeDtypeStruct((8, width), jnp.float32),
            jax.ShapeDtypeStruct((8, width), jnp.float32),
        ),
        cost_estimate=pl.CostEstimate(
            flops=work, bytes_accessed=8 * total * width, transcendentals=work // 320
        ),
        name="attend_backward",
    )(lengths, queries, keys_values, keys_values, grad_attended)


def gather_all(array):
    return lax.all_gather(array, AXES, axis=0, tiled=True)


def gather_vectors(vectors):
    packed = jnp.concatenate([vector.astype(jnp.float32) for vector in vectors])
    padded = jnp.pad(packed, (0, -packed.shape[0] % (8 * LANES)))
    every = gather_all(padded.reshape(-1, LANES)).reshape(-1, padded.shape[0])
    spread, offset = [], 0
    for vector in vectors:
        spread.append(every[:, offset : offset + vector.shape[0]].reshape(-1))
        offset += vector.shape[0]
    return spread


def scatter_vectors(vectors, count):
    sizes = [vector.shape[0] // count for vector in vectors]
    packed = jnp.concatenate(
        [vector.reshape(count, size) for vector, size in zip(vectors, sizes)], axis=1
    )
    padded = jnp.pad(packed, ((0, 0), (0, -packed.shape[1] % (8 * LANES))))
    mine = lax.psum_scatter(
        padded.reshape(-1, LANES), AXES, scatter_dimension=0, tiled=True
    ).reshape(-1)
    pieces, offset = [], 0
    for size in sizes:
        pieces.append(mine[offset : offset + size])
        offset += size
    return pieces


def scatter_weight(grad):
    return lax.psum_scatter(
        grad.astype(jnp.bfloat16), AXES, scatter_dimension=0, tiled=True
    ).astype(jnp.float32)


def on_device(
    layer_input,
    lengths,
    qkv_weight,
    qv_bias,
    out_weight,
    out_bias,
    first_gain,
    first_shift,
    up_weight,
    up_bias,
    down_weight,
    down_bias,
    second_gain,
    second_shift,
    cotangent,
):
    width = layer_input.shape[1]
    count = lax.axis_size("dp") * lax.axis_size("ctx")
    (
        bias_wide,
        out_bias_wide,
        gain_one,
        shift_one,
        up_bias_wide,
        down_bias_wide,
        gain_two,
        shift_two,
    ) = gather_vectors(
        (qv_bias, out_bias, first_gain, first_shift, up_bias, down_bias, second_gain, second_shift)
    )
    sequence = lax.all_gather(layer_input, "ctx", axis=0, tiled=True)
    full_qkv = gather_all(qkv_weight)
    full_out = gather_all(out_weight)
    full_up = gather_all(up_weight)
    full_down = gather_all(down_weight)
    weight_q = full_qkv[:, :width]
    weight_k = full_qkv[:, width : 2 * width]
    weight_v = full_qkv[:, 2 * width :]
    queries = (product(layer_input, weight_q) + bias_wide[:width]).astype(jnp.bfloat16)
    kv_bias = jnp.concatenate([jnp.zeros((width,), jnp.float32), bias_wide[width:]])
    keys_values = (product(sequence, full_qkv[:, width:]) + kv_bias).astype(jnp.bfloat16)
    attended_low = attention_forward(lengths, queries, keys_values)
    first_sum = layer_input.astype(jnp.float32) + product(attended_low, full_out) + out_bias_wide
    hidden, normed_first, inverse_first = norm_forward(first_sum, gain_one, shift_one)
    hidden_low = hidden.astype(jnp.bfloat16)
    upper = product(hidden_low, full_up) + up_bias_wide
    activation, gelu_back = jax.vjp(gelu_tanh, upper)
    activation_low = activation.astype(jnp.bfloat16)
    second_sum = hidden + product(activation_low, full_down) + down_bias_wide
    result, normed_second, inverse_second = norm_forward(second_sum, gain_two, shift_two)
    layer_output = result.astype(jnp.bfloat16)
    cot_wide = cotangent.astype(jnp.float32)
    second_shift_grad = jnp.sum(cot_wide, axis=0)
    second_gain_grad = jnp.sum(cot_wide * normed_second, axis=0)
    grad_second = norm_backward(cot_wide, normed_second, inverse_second, gain_two)
    down_bias_grad = jnp.sum(grad_second, axis=0)
    grad_second_low = grad_second.astype(jnp.bfloat16)
    down_weight_grad = scatter_weight(product_tn(activation_low, grad_second_low))
    grad_upper = gelu_back(product_nt(grad_second_low, full_down))[0]
    up_bias_grad = jnp.sum(grad_upper, axis=0)
    grad_upper_low = grad_upper.astype(jnp.bfloat16)
    up_weight_grad = scatter_weight(product_tn(hidden_low, grad_upper_low))
    grad_hidden = grad_second + product_nt(grad_upper_low, full_up)
    first_shift_grad = jnp.sum(grad_hidden, axis=0)
    first_gain_grad = jnp.sum(grad_hidden * normed_first, axis=0)
    grad_first = norm_backward(grad_hidden, normed_first, inverse_first, gain_one)
    out_bias_grad = jnp.sum(grad_first, axis=0)
    grad_first_low = grad_first.astype(jnp.bfloat16)
    out_weight_grad = scatter_weight(product_tn(attended_low, grad_first_low))
    grad_attended = product_nt(grad_first_low, full_out).astype(jnp.bfloat16)
    grad_queries, grad_keys, grad_values, query_sums, value_sums = attention_backward(
        lengths, queries, keys_values, grad_attended
    )
    qv_bias_grad = jnp.concatenate([query_sums[0], value_sums[0]])
    input_share = product_nt(grad_keys, weight_k) + product_nt(grad_values, weight_v)
    others = lax.psum_scatter(
        input_share.astype(jnp.bfloat16), "ctx", scatter_dimension=0, tiled=True
    ).astype(jnp.float32)
    qkv_weight_grad = scatter_weight(
        jnp.concatenate(
            [
                product_tn(layer_input, grad_queries),
                product_tn(sequence, grad_keys),
                product_tn(sequence, grad_values),
            ],
            axis=1,
        )
    )
    input_grad = grad_first + product_nt(grad_queries, weight_q) + others
    (
        qv_bias_grad,
        out_bias_grad,
        first_gain_grad,
        first_shift_grad,
        up_bias_grad,
        down_bias_grad,
        second_gain_grad,
        second_shift_grad,
    ) = scatter_vectors(
        (
            qv_bias_grad,
            out_bias_grad,
            first_gain_grad,
            first_shift_grad,
            up_bias_grad,
            down_bias_grad,
            second_gain_grad,
            second_shift_grad,
        ),
        count,
    )
    return (
        layer_output,
        input_grad,
        qkv_weight_grad,
        qv_bias_grad,
        out_weight_grad,
        out_bias_grad,
        first_gain_grad,
        first_shift_grad,
        up_weight_grad,
        up_bias_grad,
        down_weight_grad,
        down_bias_grad,
        second_gain_grad,
        second_shift_grad,
    )


def solution(mesh):
    placed = (
        P(("dp", "ctx"), None),
        P("dp"),
        P(("dp", "ctx"), None),
        P(("dp", "ctx")),
        P(("dp", "ctx"), None),
        P(("dp", "ctx")),
        P(("dp", "ctx")),
        P(("dp", "ctx")),
        P(("dp", "ctx"), None),
        P(("dp", "ctx")),
        P(("dp", "ctx"), None),
        P(("dp", "ctx")),
        P(("dp", "ctx")),
        P(("dp", "ctx")),
        P(("dp", "ctx"), None),
    )
    return jax.shard_map(
        on_device,
        mesh=mesh,
        in_specs=placed,
        out_specs=(
            P(("dp", "ctx"), None),
            P(("dp", "ctx"), None),
            P(("dp", "ctx"), None),
            P(("dp", "ctx")),
            P(("dp", "ctx"), None),
            P(("dp", "ctx")),
            P(("dp", "ctx")),
            P(("dp", "ctx")),
            P(("dp", "ctx"), None),
            P(("dp", "ctx")),
            P(("dp", "ctx"), None),
            P(("dp", "ctx")),
            P(("dp", "ctx")),
            P(("dp", "ctx")),
        ),
        check_vma=False,
    )
```

```python
import jax
import jax.numpy as jnp
from jax import lax
from jax.experimental import pallas as pl
from jax.experimental.pallas import tpu as pltpu
from jax.sharding import PartitionSpec as P

HEAD_DIM = 64


EPSILON = 1e-05


def gelu_tanh(value):
    return (
        0.5
        * value
        * (1.0 + jnp.tanh(0.7978845608028654 * (value + 0.044715 * value * value * value)))
    )


def product(left, right):
    return jnp.dot(left, right, preferred_element_type=jnp.float32)


def product_tn(left, right):
    return lax.dot_general(
        left, right, (((0,), (0,)), ((), ())), preferred_element_type=jnp.float32
    )


def product_nt(left, right):
    return lax.dot_general(
        left, right, (((1,), (1,)), ((), ())), preferred_element_type=jnp.float32
    )


def norm_forward(rows, gain, shift):
    centered = rows - jnp.mean(rows, axis=-1, keepdims=True)
    inverse = lax.rsqrt(jnp.mean(centered * centered, axis=-1, keepdims=True) + EPSILON)
    normed = centered * inverse
    return (normed * gain + shift, normed, inverse)


def norm_backward(grad_rows, normed, inverse, gain):
    scaled = grad_rows * gain
    return inverse * (
        scaled
        - jnp.mean(scaled, axis=-1, keepdims=True)
        - normed * jnp.mean(scaled * normed, axis=-1, keepdims=True)
    )


LANES = 128
AXES = ("dp", "ctx")


def head_scores(query, key, limit):
    scores = product_nt(query, key) * HEAD_DIM ** (-0.5)
    position = lax.broadcasted_iota(jnp.int32, scores.shape, 1)
    return jnp.where(position < limit, scores, -jnp.inf)


def log_sum(scores):
    peak = jnp.max(scores, axis=-1, keepdims=True)
    return peak + jnp.log(jnp.sum(jnp.exp(scores - peak), axis=-1, keepdims=True))


def forward_kernel(length_ref, query_ref, key_ref, value_ref, out_ref):
    limit = length_ref[0]
    for head in range(LANES // HEAD_DIM):
        span = slice(head * HEAD_DIM, (head + 1) * HEAD_DIM)
        scores = head_scores(query_ref[:, span], key_ref[:, span], limit)
        weights = jnp.exp(scores - log_sum(scores)).astype(jnp.bfloat16)
        out_ref[:, span] = product(weights, value_ref[:, span]).astype(jnp.bfloat16)


def backward_kernel(
    length_ref, query_ref, key_ref, value_ref, grad_ref, gq_ref, gk_ref, gv_ref, qsum_ref, vsum_ref
):
    limit = length_ref[0]
    scale = HEAD_DIM ** (-0.5)
    for head in range(LANES // HEAD_DIM):
        span = slice(head * HEAD_DIM, (head + 1) * HEAD_DIM)
        query, key, value = query_ref[:, span], key_ref[:, span], value_ref[:, span]
        grad = grad_ref[:, span]
        scores = head_scores(query, key, limit)
        probs = jnp.exp(scores - log_sum(scores))
        grad_probs = product_nt(grad, value)
        inner = jnp.sum(probs * grad_probs, axis=-1, keepdims=True)
        grad_low = (probs * (grad_probs - inner)).astype(jnp.bfloat16)
        grad_query = product(grad_low, key) * scale
        gq_ref[:, span] = grad_query.astype(jnp.bfloat16)
        gk_ref[:, span] = (product_tn(grad_low, query) * scale).astype(jnp.bfloat16)
        grad_value = product_tn(probs.astype(jnp.bfloat16), grad)
        gv_ref[:, span] = grad_value.astype(jnp.bfloat16)
        qsum_ref[:, span] = jnp.broadcast_to(
            jnp.sum(grad_query, axis=0, keepdims=True), (8, HEAD_DIM)
        )
        vsum_ref[:, span] = jnp.broadcast_to(
            jnp.sum(grad_value, axis=0, keepdims=True), (8, HEAD_DIM)
        )


def attention_specs(rows, total):
    local = pl.BlockSpec((rows, LANES), lambda p: (0, p))
    return (
        pl.BlockSpec(memory_space=pltpu.SMEM),
        local,
        pl.BlockSpec((total, LANES), lambda p: (0, p)),
        pl.BlockSpec((total, LANES), lambda p: (0, p)),
    )


def attention_forward(lengths, queries, keys, values):
    rows, width = queries.shape
    total, pairs = keys.shape[0], width // LANES
    work = 4 * rows * total * width
    return pl.pallas_call(
        forward_kernel,
        grid=(pairs,),
        in_specs=attention_specs(rows, total),
        out_specs=pl.BlockSpec((rows, LANES), lambda p: (0, p)),
        out_shape=jax.ShapeDtypeStruct((rows, width), jnp.bfloat16),
        cost_estimate=pl.CostEstimate(
            flops=work, bytes_accessed=4 * total * width, transcendentals=work // 64
        ),
        name="attend_forward",
    )(lengths, queries, keys, values)


def attention_backward(lengths, queries, keys, values, grad_attended):
    rows, width = queries.shape
    total, pairs = keys.shape[0], width // LANES
    work = 10 * rows * total * width
    local = pl.BlockSpec((rows, LANES), lambda p: (0, p))
    long = pl.BlockSpec((total, LANES), lambda p: (0, p))
    short = pl.BlockSpec((8, LANES), lambda p: (0, p))
    return pl.pallas_call(
        backward_kernel,
        grid=(pairs,),
        in_specs=(*attention_specs(rows, total), local),
        out_specs=(local, long, long, short, short),
        out_shape=(
            jax.ShapeDtypeStruct((rows, width), jnp.bfloat16),
            jax.ShapeDtypeStruct((total, width), jnp.bfloat16),
            jax.ShapeDtypeStruct((total, width), jnp.bfloat16),
            jax.ShapeDtypeStruct((8, width), jnp.float32),
            jax.ShapeDtypeStruct((8, width), jnp.float32),
        ),
        cost_estimate=pl.CostEstimate(
            flops=work, bytes_accessed=8 * total * width, transcendentals=work // 320
        ),
        name="attend_backward",
    )(lengths, queries, keys, values, grad_attended)


def row_blocks(array, width):
    return [array[:, start : start + width] for start in range(0, array.shape[1], width)]


def gather_parameters(weights, vectors, width):
    packed = jnp.concatenate(vectors)
    packed = jnp.pad(packed, (0, -packed.shape[0] % width)).reshape(-1, width)
    rows = jnp.concatenate([b for w in weights for b in row_blocks(w, width)] + [packed], axis=0)
    rows = jnp.pad(rows, ((0, -rows.shape[0] % 8), (0, 0)))
    every = lax.all_gather(rows, AXES, axis=0)
    full, offset = [], 0
    for weight in weights:
        blocks = []
        for _ in range(weight.shape[1] // width):
            block = every[:, offset : offset + weight.shape[0]]
            blocks.append(block.reshape(-1, width))
            offset += weight.shape[0]
        full.append(blocks)
    flat = every[:, offset : offset + packed.shape[0]].reshape(every.shape[0], -1)
    flat = flat.astype(jnp.float32)
    spread, offset = [], 0
    for vector in vectors:
        spread.append(flat[:, offset : offset + vector.shape[0]].reshape(-1))
        offset += vector.shape[0]
    return full, spread


def scatter_gradients(weights, vectors, count, width):
    low = jnp.bfloat16
    sizes = [vector.shape[0] // count for vector in vectors]
    packed = jnp.concatenate(
        [vector.reshape(count, size) for vector, size in zip(vectors, sizes)], axis=1
    ).astype(low)
    packed = jnp.pad(packed, ((0, 0), (0, -packed.shape[1] % width))).reshape(count, -1, width)
    blocks = [block.astype(low).reshape(count, -1, width) for w in weights for block in w]
    rows = jnp.concatenate(blocks + [packed], axis=1)
    rows = jnp.pad(rows, ((0, 0), (0, -rows.shape[1] % 8), (0, 0)))
    depth = rows.shape[1]
    mine = lax.psum_scatter(
        rows.reshape(count * depth, width), AXES, scatter_dimension=0, tiled=True
    ).astype(jnp.float32)
    summed, offset = [], 0
    for weight in weights:
        pieces = []
        for block in weight:
            owned = block.shape[0] // count
            pieces.append(mine[offset : offset + owned])
            offset += owned
        summed.append(jnp.concatenate(pieces, axis=1))
    flat = mine[offset : offset + packed.shape[1]].reshape(-1)
    parts, offset = [], 0
    for size in sizes:
        parts.append(flat[offset : offset + size])
        offset += size
    return summed, parts


def on_device(
    layer_input,
    lengths,
    qkv_weight,
    qv_bias,
    out_weight,
    out_bias,
    first_gain,
    first_shift,
    up_weight,
    up_bias,
    down_weight,
    down_bias,
    second_gain,
    second_shift,
    cotangent,
):
    width = layer_input.shape[1]
    count = lax.axis_size("dp") * lax.axis_size("ctx")
    sequence = lax.all_gather(layer_input, "ctx", axis=0, tiled=True)
    (
        ((weight_q, weight_k, weight_v), (full_out,), up_blocks, (full_down,)),
        (
            bias_wide,
            out_bias_wide,
            gain_one,
            shift_one,
            up_bias_wide,
            down_bias_wide,
            gain_two,
            shift_two,
        ),
    ) = gather_parameters(
        (qkv_weight, out_weight, up_weight, down_weight),
        (qv_bias, out_bias, first_gain, first_shift, up_bias, down_bias, second_gain, second_shift),
        width,
    )
    full_up = jnp.concatenate(up_blocks, axis=1)
    queries = (product(layer_input, weight_q) + bias_wide[:width]).astype(jnp.bfloat16)
    keys = product(sequence, weight_k).astype(jnp.bfloat16)
    values = (product(sequence, weight_v) + bias_wide[width:]).astype(jnp.bfloat16)
    attended_low = attention_forward(lengths, queries, keys, values)
    first_sum = layer_input.astype(jnp.float32) + product(attended_low, full_out) + out_bias_wide
    hidden, normed_first, inverse_first = norm_forward(first_sum, gain_one, shift_one)
    hidden_low = hidden.astype(jnp.bfloat16)
    upper = product(hidden_low, full_up) + up_bias_wide
    activation, gelu_back = jax.vjp(gelu_tanh, upper)
    activation_low = activation.astype(jnp.bfloat16)
    second_sum = hidden + product(activation_low, full_down) + down_bias_wide
    result, normed_second, inverse_second = norm_forward(second_sum, gain_two, shift_two)
    layer_output = result.astype(jnp.bfloat16)
    cot_wide = cotangent.astype(jnp.float32)
    second_shift_grad = jnp.sum(cot_wide, axis=0)
    second_gain_grad = jnp.sum(cot_wide * normed_second, axis=0)
    grad_second = norm_backward(cot_wide, normed_second, inverse_second, gain_two)
    down_bias_grad = jnp.sum(grad_second, axis=0)
    grad_second_low = grad_second.astype(jnp.bfloat16)
    down_weight_grad = product_tn(activation_low, grad_second_low)
    grad_upper = gelu_back(product_nt(grad_second_low, full_down))[0]
    up_bias_grad = jnp.sum(grad_upper, axis=0)
    grad_upper_low = grad_upper.astype(jnp.bfloat16)
    up_weight_grad = product_tn(hidden_low, grad_upper_low)
    grad_hidden = grad_second + product_nt(grad_upper_low, full_up)
    first_shift_grad = jnp.sum(grad_hidden, axis=0)
    first_gain_grad = jnp.sum(grad_hidden * normed_first, axis=0)
    grad_first = norm_backward(grad_hidden, normed_first, inverse_first, gain_one)
    out_bias_grad = jnp.sum(grad_first, axis=0)
    grad_first_low = grad_first.astype(jnp.bfloat16)
    out_weight_grad = product_tn(attended_low, grad_first_low)
    grad_attended = product_nt(grad_first_low, full_out).astype(jnp.bfloat16)
    grad_queries, grad_keys, grad_values, query_sums, value_sums = attention_backward(
        lengths, queries, keys, values, grad_attended
    )
    qv_bias_grad = jnp.concatenate([query_sums[0], value_sums[0]])
    input_share = product_nt(grad_keys, weight_k) + product_nt(grad_values, weight_v)
    others = lax.psum_scatter(
        input_share.astype(jnp.bfloat16), "ctx", scatter_dimension=0, tiled=True
    ).astype(jnp.float32)
    qkv_blocks = (
        product_tn(layer_input, grad_queries),
        product_tn(sequence, grad_keys),
        product_tn(sequence, grad_values),
    )
    input_grad = grad_first + product_nt(grad_queries, weight_q) + others
    (
        (qkv_weight_grad, out_weight_grad, up_weight_grad, down_weight_grad),
        (
            qv_bias_grad,
            out_bias_grad,
            first_gain_grad,
            first_shift_grad,
            up_bias_grad,
            down_bias_grad,
            second_gain_grad,
            second_shift_grad,
        ),
    ) = scatter_gradients(
        (
            qkv_blocks,
            (out_weight_grad,),
            row_blocks(up_weight_grad, width),
            (down_weight_grad,),
        ),
        (
            qv_bias_grad,
            out_bias_grad,
            first_gain_grad,
            first_shift_grad,
            up_bias_grad,
            down_bias_grad,
            second_gain_grad,
            second_shift_grad,
        ),
        count,
        width,
    )
    return (
        layer_output,
        input_grad,
        qkv_weight_grad,
        qv_bias_grad,
        out_weight_grad,
        out_bias_grad,
        first_gain_grad,
        first_shift_grad,
        up_weight_grad,
        up_bias_grad,
        down_weight_grad,
        down_bias_grad,
        second_gain_grad,
        second_shift_grad,
    )


def solution(mesh):
    placed = (
        P(("dp", "ctx"), None),
        P("dp"),
        P(("dp", "ctx"), None),
        P(("dp", "ctx")),
        P(("dp", "ctx"), None),
        P(("dp", "ctx")),
        P(("dp", "ctx")),
        P(("dp", "ctx")),
        P(("dp", "ctx"), None),
        P(("dp", "ctx")),
        P(("dp", "ctx"), None),
        P(("dp", "ctx")),
        P(("dp", "ctx")),
        P(("dp", "ctx")),
        P(("dp", "ctx"), None),
    )
    return jax.shard_map(
        on_device,
        mesh=mesh,
        in_specs=placed,
        out_specs=(
            P(("dp", "ctx"), None),
            P(("dp", "ctx"), None),
            P(("dp", "ctx"), None),
            P(("dp", "ctx")),
            P(("dp", "ctx"), None),
            P(("dp", "ctx")),
            P(("dp", "ctx")),
            P(("dp", "ctx")),
            P(("dp", "ctx"), None),
            P(("dp", "ctx")),
            P(("dp", "ctx"), None),
            P(("dp", "ctx")),
            P(("dp", "ctx")),
            P(("dp", "ctx")),
        ),
        check_vma=False,
    )
```
